128 devices in a mesh: prow: 16 (over x, z_hi, core), pcol: 8 (over z_lo, y).
Axes of the slice: x: 4, y: 4, z: 4 (z_hi: 2, z_lo: 2; z = z_hi * 2 + z_lo), core: 2. Of those that a mesh axis runs over, the one named last changes fastest.
Arguments:
- inverse: bfloat16 [4, 8192, 8, 4096], P(None, 'prow', None, 'pcol'), may hold values from -6 to 6
- panel: bfloat16 [2, 4, 8192, 256], P(None, None, 'prow'), may hold values from -0.0625 to 0.0625
- structure: int32 [2, 16], replicated, may hold values from 0 to 63, as said below
- diag_inverse: float32 [2, 256, 256], replicated, may hold values from -6 to 6
Outputs:
- off_diag: bfloat16 [2, 4, 8192, 256], P(None, None, ('prow', 'pcol'))
- diag_block: float32 [2, 256, 256], replicated
The draws below stay inside these ranges and needn't reach their ends.
Inputs may be any that keep to these rules, and one draw needn't show every extreme that they name: `structure`: each row lists 16 distinct block indices in increasing order, exactly one of them congruent to p modulo 16 for every p, and always includes the last ancestor block 63.
All inputs are finite; a program needn't handle non-finite values.
Results may differ from the reference program's by a relative error of at most 0.0022.
Values may be sent and summed in bfloat16 or wider, within the bound.
No kernel may reach another device: no remote copies, remote signals or barrier semaphores. Data moves between devices by JAX's collectives and lax.ppermute only.
A program may use at most 128 MiB of HBM per device.

```python
import jax
import jax.numpy as jnp

BLK = 512
W = 256
NODES = 2
BR_DEV = 4
BC_DEV = 8
SEL = 16
N_PROW = 16
N_PCOL = 8


def draw_structure(key, part):
    listed = []
    for supernode in range(NODES):
        subkey = jax.random.fold_in(key, 17 + supernode)
        offsets = jax.random.randint(subkey, (SEL,), 0, BR_DEV).astype(jnp.int32)
        offsets = offsets.at[SEL - 1].set(BR_DEV - 1)
        indices = offsets * SEL + jnp.arange(SEL, dtype=jnp.int32)
        listed.append(jnp.sort(indices))
    return jnp.stack(listed).astype(jnp.int32)


def block_levels(rng, extent, cuts, smallest, largest):
    level = 1.0
    for position, shards_of in cuts:
        heights = jax.random.uniform(jax.random.fold_in(jax.random.fold_in(rng, 6), position), (shards_of,), jnp.float32, smallest / len(cuts), largest / len(cuts))
        level = level * jnp.repeat(jnp.exp(heights), extent[position] // shards_of).reshape((-1,) + (1,) * (len(extent) - 1 - position))
    return level


def bell_draw(stream_key, extent, spread, bound, cuts=(), kind=jnp.bfloat16):
    array = spread * jax.random.normal(stream_key, extent, jnp.float32)
    if cuts:
        array = array * block_levels(stream_key, extent, cuts, -0.22, 0.18)
    return jnp.clip(array, -bound, bound).astype(kind)


def setup_inputs(seed: int = 0) -> dict:
    key_of = jax.random.split(jax.random.key(seed), 5)
    inverse = bell_draw(key_of[0], (BR_DEV, N_PROW * BLK, BC_DEV, N_PCOL * BLK), 1.0, 6.0, ((1, 16), (3, 8)))
    panel = bell_draw(key_of[1], (NODES, BR_DEV, N_PROW * BLK, W), (SEL * BLK) ** -0.5, 0.0625, ((2, 16),))
    structure = draw_structure(jax.random.fold_in(key_of[4], 71), 0)
    diag_inverse = bell_draw(key_of[3], (NODES, W, W), 1.0, 6.0, (), jnp.float32)
    return {"inverse": inverse, "panel": panel, "structure": structure, "diag_inverse": diag_inverse}


def reference(inverse, panel, structure, diag_inverse):
    total_blocks = BR_DEV * N_PROW
    blocks = inverse.reshape(total_blocks, BLK, total_blocks, BLK)
    pieces = []
    products = []
    for supernode in range(NODES):
        chosen = structure[supernode]
        factor_blocks = panel[supernode].reshape(total_blocks, BLK, W)
        factor_rows = jnp.take(factor_blocks, chosen, axis=0).reshape(SEL * BLK, W)
        picked = jnp.take(jnp.take(blocks, chosen, axis=0), chosen, axis=2).reshape(SEL * BLK, SEL * BLK)
        result = (-jnp.dot(picked, factor_rows, preferred_element_type=jnp.float32)).astype(jnp.bfloat16)
        placed = jnp.zeros((total_blocks, BLK, W), jnp.bfloat16).at[chosen].set(result.reshape(SEL, BLK, W))
        pieces.append(placed.reshape(BR_DEV, N_PROW * BLK, W))
        products.append(jnp.dot(factor_rows.T, result, preferred_element_type=jnp.float32))
    return jnp.stack(pieces), diag_inverse - jnp.stack(products)
```

```python
import functools

import jax
import jax.numpy as jnp
from jax import lax
from jax.experimental import pallas as pl
from jax.experimental.pallas import tpu as pltpu
from jax.sharding import PartitionSpec as P

BOTH = ("prow", "pcol")
SMEM = pl.BlockSpec(memory_space=pltpu.SMEM)
VMEM = pl.BlockSpec(memory_space=pltpu.VMEM)
ANY = pl.BlockSpec(memory_space=pl.ANY)
HBM = pl.BlockSpec(memory_space=pltpu.HBM)
VMEM_LIMIT = 48 * 1024 * 1024
SHIFT = (2, 0, 1, 3)


def spread():
    pairs = []
    for row in range(16):
        x, z_hi, core = row // 4, row // 2 % 2, row % 2
        for col in range(8):
            z_lo, y = col // 4, col % 4
            to_x = (x + SHIFT[(y - (z_hi * 2 + core)) % 4]) % 4
            to_z_hi = z_hi if z_lo == x % 2 else 1 - z_hi
            to_row = (to_x * 2 + to_z_hi) * 2 + x // 2
            pairs.append((row * 8 + col, to_row * 8 + row % 8))
    return pairs


SPREAD = spread()
SWAP = [(row, row ^ 1) for row in range(16)]
SAME_CORE = [[row for row in range(16) if row % 2 == core] for core in range(2)]


def pick_blocks(structure, panel, picks, chosen, sems):
    row, col = lax.axis_index("prow"), lax.axis_index("pcol")
    core = row & 1
    wanted = (row, col + 8 * core, col + 8 * (1 - core))
    copies = []
    for s in range(2):
        found = [jnp.int32(0)] * 3
        for k in range(16):
            entry = structure[s, k]
            for i in range(3):
                found[i] += jnp.where((entry & 15) == wanted[i], entry >> 4, 0)
        copies.append(pltpu.make_async_copy(panel.at[s, found[0]], chosen.at[s], sems.at[s]))
        copies[-1].start()
        picks[s, 0] = found[0]
        picks[s, 1] = 2 * found[1] + core
        picks[s, 2] = 2 * found[2] + 1 - core
    for copy in copies:
        copy.wait()


def extract(picks, block, out, wide):
    s = pl.program_id(0)
    rows = block.shape[1]
    for k in range(4):
        lanes = slice(128 * k, 128 * k + 128)
        wide[k] = block[0, :, :, lanes].astype(jnp.float32).reshape(rows * 8, 128)
        for i in range(2):
            column = wide[k, pl.ds(picks[s, 1 + i], rows, stride=8), :]
            out[0, i, :, lanes] = column.astype(jnp.bfloat16)


def multiply(blocks, own, other, out):
    for s in range(2):
        total = None
        for i, factor in enumerate((own, other)):
            term = lax.dot_general(
                factor[s], blocks[s, i], (((0,), (1,)), ((), ())), preferred_element_type=jnp.float32
            )
            total = term if total is None else total + term
        out[:, s] = (-total).reshape(8, 32, 512)


def round_and_project(arrived, chosen, columns, kept, sent):
    core = lax.axis_index("prow") & 1
    for s in range(2):
        total = arrived[0, s]
        for i in range(1, 8):
            total += arrived[i, s]
        rounded = total.astype(jnp.bfloat16)
        columns[s] = rounded
        term = jnp.dot(rounded, chosen[s], preferred_element_type=jnp.float32)
        first = core == 0
        kept[s] = jnp.where(first, term[:16], term[16:])
        sent[s] = jnp.where(first, term[16:], term[:16])


def pair_sum(kept, arrived, out):
    total = kept[...] + arrived[...]
    for i in range(8):
        out[i] = total


def pack(arrived, columns, out):
    for s in range(2):
        total = arrived[0, s]
        for i in range(1, 8):
            total += arrived[i, s]
        high = total.astype(jnp.bfloat16)
        low = (total - high.astype(jnp.float32)).astype(jnp.bfloat16)
        for i in range(8):
            out[i, 32 * s : 32 * s + 16] = high
            out[i, 32 * s + 16 : 32 * s + 32] = low
            out[i, 64:, 128 * s : 128 * s + 128] = columns[s, :, i // 2 * 128 : i // 2 * 128 + 128]


def finish(picks, own, other, diag_inverse, off_diag, diag_block):
    core = lax.axis_index("prow") & 1
    half = lax.axis_index("pcol") & 1
    off_diag[...] = jnp.zeros_like(off_diag)
    for s in range(2):
        slabs = []
        for i in range(8):
            high, low = (slice(32 * s + 16 * k, 32 * s + 16 * k + 16) for k in range(2))
            mine = own[i, high].astype(jnp.float32) + own[i, low].astype(jnp.float32)
            theirs = other[i, high].astype(jnp.float32) + other[i, low].astype(jnp.float32)
            slabs.append(jnp.where(core == 0, mine, theirs))
            slabs.append(jnp.where(core == 0, theirs, mine))
        diag_block[s] = diag_inverse[s] - jnp.concatenate(slabs, axis=0).T
        part = jnp.concatenate(
            [own[i, 64:, 128 * s : 128 * s + 128].astype(jnp.float32) for i in range(8)], axis=0
        ).T
        rows = jnp.where(half == 0, part[:64], part[64:])
        off_diag[s, picks[s, 0]] = rows.astype(jnp.bfloat16)


def call(body, out_shape, **rest):
    return pl.pallas_call(
        body,
        out_shape=out_shape,
        compiler_params=pltpu.CompilerParams(vmem_limit_bytes=VMEM_LIMIT),
        **rest,
    )


def on_device(inverse, panel, structure, diag_inverse):
    f32, bf16 = jnp.float32, jnp.bfloat16
    shape = jax.ShapeDtypeStruct
    picks, chosen = call(
        pick_blocks,
        (shape((2, 3), jnp.int32), shape((2, 512, 256), bf16)),
        in_specs=[SMEM, HBM],
        out_specs=(SMEM, ANY),
        scratch_shapes=[pltpu.SemaphoreType.DMA((2,))],
    )(structure, panel)
    own = lax.ppermute(chosen, BOTH, SPREAD)
    rows = 128
    blocks = call(
        extract,
        shape((2, 2, 512, 512), bf16),
        grid_spec=pltpu.PrefetchScalarGridSpec(
            num_scalar_prefetch=1,
            grid=(2, 512 // rows),
            in_specs=[pl.BlockSpec((1, rows, 8, 512), lambda s, i, picks: (picks[s, 0], i, 0, 0))],
            out_specs=pl.BlockSpec((1, 2, rows, 512), lambda s, i, picks: (s, 0, i, 0)),
            scratch_shapes=[pltpu.VMEM((4, rows * 8, 128), f32)],
        ),
        cost_estimate=pl.CostEstimate(flops=0, bytes_accessed=10 << 20, transcendentals=0),
    )(picks, inverse)
    own, blocks = lax.optimization_barrier((own, blocks))
    other = lax.ppermute(own, "prow", SWAP)
    partial = call(
        multiply,
        shape((8, 2, 32, 512), f32),
        in_specs=[VMEM, VMEM, VMEM],
        out_specs=VMEM,
    )(blocks, own, other)
    arrived = lax.all_to_all(partial, "pcol", 0, 0)
    columns, kept, sent = call(
        round_and_project,
        (shape((2, 32, 512), bf16), shape((2, 16, 256), f32), shape((2, 16, 256), f32)),
        in_specs=[VMEM, VMEM],
        out_specs=(VMEM, VMEM, VMEM),
    )(arrived, chosen)
    copies = call(
        pair_sum, shape((8, 2, 16, 256), f32), in_specs=[VMEM, VMEM], out_specs=VMEM
    )(kept, lax.ppermute(sent, "prow", SWAP))
    sums = lax.all_to_all(copies, "prow", 0, 0, axis_index_groups=SAME_CORE)
    packed = call(
        pack, shape((8, 96, 256), bf16), in_specs=[VMEM, VMEM], out_specs=VMEM
    )(sums, columns)
    final = lax.all_to_all(packed, "pcol", 0, 0)
    sibling = lax.ppermute(final[:, :64], "prow", SWAP)
    return call(
        finish,
        (shape((2, 4, 64, 256), bf16), shape((2, 256, 256), f32)),
        in_specs=[SMEM, VMEM, VMEM, VMEM],
        out_specs=(VMEM, VMEM),
    )(picks, final, sibling, diag_inverse)


def solution(mesh):
    placed = (P(None, "prow", None, "pcol"), P(None, None, "prow", None), P(), P())
    return jax.shard_map(
        on_device,
        mesh=mesh,
        in_specs=placed,
        out_specs=(P(None, None, ("prow", "pcol"), None), P()),
        check_vma=False,
    )
```

```python
import functools

import jax
import jax.numpy as jnp
from jax import lax
from jax.experimental import pallas as pl
from jax.experimental.pallas import tpu as pltpu
from jax.sharding import PartitionSpec as P

BOTH = ("prow", "pcol")
SMEM = pl.BlockSpec(memory_space=pltpu.SMEM)
VMEM = pl.BlockSpec(memory_space=pltpu.VMEM)
ANY = pl.BlockSpec(memory_space=pl.ANY)
HBM = pl.BlockSpec(memory_space=pltpu.HBM)
VMEM_LIMIT = 48 * 1024 * 1024
SHIFT = (2, 0, 1, 3)


def spread():
    pairs = []
    for row in range(16):
        x, z_hi, core = row // 4, row // 2 % 2, row % 2
        for col in range(8):
            z_lo, y = col // 4, col % 4
            to_x = (x + SHIFT[(y - (z_hi * 2 + core)) % 4]) % 4
            to_z_hi = z_hi if z_lo == x % 2 else 1 - z_hi
            to_row = (to_x * 2 + to_z_hi) * 2 + x // 2
            pairs.append((row * 8 + col, to_row * 8 + row % 8))
    return pairs


SPREAD = spread()
SWAP = [(row, row ^ 1) for row in range(16)]
SAME_CORE = [[row for row in range(16) if row % 2 == core] for core in range(2)]


def pick_blocks(listed, panel, picks, chosen, structure, sems):
    fetch = pltpu.make_async_copy(listed, structure, sems.at[0])
    fetch.start()
    fetch.wait()
    row, col = lax.axis_index("prow"), lax.axis_index("pcol")
    core = row & 1
    wanted = (row, col + 8 * core, col + 8 * (1 - core))
    copies = []
    for s in range(2):
        found = [jnp.int32(0)] * 3
        for k in range(16):
            entry = structure[s, k]
            for i in range(3):
                found[i] += jnp.where((entry & 15) == wanted[i], entry >> 4, 0)
        copies.append(pltpu.make_async_copy(panel.at[s, found[0]], chosen.at[s], sems.at[s]))
        copies[-1].start()
        picks[s, 0] = found[0]
        picks[s, 1] = 2 * found[1] + core
        picks[s, 2] = 2 * found[2] + 1 - core
    for copy in copies:
        copy.wait()


def extract(picks, block, out, wide):
    s = pl.program_id(0)
    rows = block.shape[1]
    for k in range(4):
        lanes = slice(128 * k, 128 * k + 128)
        wide[k] = block[0, :, :, lanes].astype(jnp.float32).reshape(rows * 8, 128)
        for i in range(2):
            column = wide[k, pl.ds(picks[s, 1 + i], rows, stride=8), :]
            out[0, i, :, lanes] = column.astype(jnp.bfloat16)


def multiply(blocks, own, other, out):
    for s in range(2):
        total = None
        for i, factor in enumerate((own, other)):
            term = lax.dot_general(
                factor[s], blocks[s, i], (((0,), (1,)), ((), ())), preferred_element_type=jnp.float32
            )
            total = term if total is None else total + term
        for d in range(8):
            piece = -total[32 * d : 32 * d + 32]
            largest = jnp.max(jnp.max(jnp.abs(piece), axis=0, keepdims=True), axis=1, keepdims=True)
            exponent = jnp.ceil(jnp.log2(jnp.maximum(largest, 2.0**-120)))
            scaled = jnp.clip(piece * jnp.exp2(-exponent) * 32767.0, -32767.0, 32767.0)
            coded = jnp.round(scaled).astype(jnp.int32).astype(jnp.int16)
            for k in range(4):
                row = 64 * k + 32 * s
                out[d, row : row + 32] = coded[:, 128 * k : 128 * k + 128]
            tail = jnp.broadcast_to(exponent, (16, 128)).astype(jnp.int32).astype(jnp.int16)
            out[d, 256 + 16 * s : 272 + 16 * s] = tail


def round_and_project(arrived, chosen, columns, kept, sent):
    core = lax.axis_index("prow") & 1
    for s in range(2):
        total = [jnp.zeros((32, 128), jnp.float32)] * 4
        for i in range(8):
            tail = arrived[i, 256 + 16 * s : 272 + 16 * s].astype(jnp.int32).astype(jnp.float32)
            scale = jnp.exp2(tail[:1]) * (1 / 32767.0)
            for k in range(4):
                row = 64 * k + 32 * s
                coded = arrived[i, row : row + 32].astype(jnp.int32).astype(jnp.float32)
                total[k] += coded * scale
        rounded = jnp.concatenate(total, axis=1).astype(jnp.bfloat16)
        columns[s] = rounded
        term = jnp.dot(rounded, chosen[s], preferred_element_type=jnp.float32)
        first = core == 0
        kept[s] = jnp.where(first, term[:16], term[16:])
        sent[s] = jnp.where(first, term[16:], term[:16])


def pair_sum(kept, arrived, out):
    total = kept[...] + arrived[...]
    for i in range(8):
        out[i] = total


def pack(arrived, columns, out):
    for s in range(2):
        total = arrived[0, s]
        for i in range(1, 8):
            total += arrived[i, s]
        high = total.astype(jnp.bfloat16)
        low = (total - high.astype(jnp.float32)).astype(jnp.bfloat16)
        for i in range(8):
            out[i, 32 * s : 32 * s + 16] = high
            out[i, 32 * s + 16 : 32 * s + 32] = low
            out[i, 64:, 128 * s : 128 * s + 128] = columns[s, :, i // 2 * 128 : i // 2 * 128 + 128]


def finish(picks, own, other, diag_inverse, off_diag, diag_block):
    core = lax.axis_index("prow") & 1
    half = lax.axis_index("pcol") & 1
    off_diag[...] = jnp.zeros_like(off_diag)
    for s in range(2):
        slabs = []
        for i in range(8):
            high, low = (slice(32 * s + 16 * k, 32 * s + 16 * k + 16) for k in range(2))
            mine = own[i, high].astype(jnp.float32) + own[i, low].astype(jnp.float32)
            theirs = other[i, high].astype(jnp.float32) + other[i, low].astype(jnp.float32)
            slabs.append(jnp.where(core == 0, mine, theirs))
            slabs.append(jnp.where(core == 0, theirs, mine))
        diag_block[s] = diag_inverse[s] - jnp.concatenate(slabs, axis=0).T
        part = jnp.concatenate(
            [own[i, 64:, 128 * s : 128 * s + 128].astype(jnp.float32) for i in range(8)], axis=0
        ).T
        rows = jnp.where(half == 0, part[:64], part[64:])
        off_diag[s, picks[s, 0]] = rows.astype(jnp.bfloat16)


def call(body, out_shape, limit=VMEM_LIMIT, **rest):
    return pl.pallas_call(
        body,
        out_shape=out_shape,
        compiler_params=pltpu.CompilerParams(vmem_limit_bytes=limit),
        **rest,
    )


def on_device(inverse, panel, structure, diag_inverse):
    f32, bf16 = jnp.float32, jnp.bfloat16
    shape = jax.ShapeDtypeStruct
    picks, chosen = call(
        pick_blocks,
        (shape((2, 3), jnp.int32), shape((2, 512, 256), bf16)),
        in_specs=[HBM, HBM],
        out_specs=(SMEM, ANY),
        scratch_shapes=[pltpu.SMEM((2, 16), jnp.int32), pltpu.SemaphoreType.DMA((2,))],
        limit=62 * 1024 * 1024,
    )(structure, panel)
    own = lax.ppermute(chosen, BOTH, SPREAD)
    rows = 128
    blocks = call(
        extract,
        shape((2, 2, 512, 512), bf16),
        grid_spec=pltpu.PrefetchScalarGridSpec(
            num_scalar_prefetch=1,
            grid=(2, 512 // rows),
            in_specs=[pl.BlockSpec((1, rows, 8, 512), lambda s, i, picks: (picks[s, 0], i, 0, 0))],
            out_specs=pl.BlockSpec((1, 2, rows, 512), lambda s, i, picks: (s, 0, i, 0)),
            scratch_shapes=[pltpu.VMEM((4, rows * 8, 128), f32)],
        ),
        cost_estimate=pl.CostEstimate(flops=0, bytes_accessed=10 << 20, transcendentals=0),
    )(picks, inverse)
    own, blocks = lax.optimization_barrier((own, blocks))
    other = lax.ppermute(own, "prow", SWAP)
    partial = call(
        multiply,
        shape((8, 288, 128), jnp.int16),
        in_specs=[VMEM, VMEM, VMEM],
        out_specs=VMEM,
    )(blocks, own, other)
    arrived = lax.all_to_all(partial, "pcol", 0, 0)
    columns, kept, sent = call(
        round_and_project,
        (shape((2, 32, 512), bf16), shape((2, 16, 256), f32), shape((2, 16, 256), f32)),
        in_specs=[VMEM, VMEM],
        out_specs=(VMEM, VMEM, VMEM),
    )(arrived, chosen)
    copies = call(
        pair_sum, shape((8, 2, 16, 256), f32), in_specs=[VMEM, VMEM], out_specs=VMEM
    )(kept, lax.ppermute(sent, "prow", SWAP))
    sums = lax.all_to_all(copies, "prow", 0, 0, axis_index_groups=SAME_CORE)
    packed = call(
        pack, shape((8, 96, 256), bf16), in_specs=[VMEM, VMEM], out_specs=VMEM
    )(sums, columns)
    final = lax.all_to_all(packed, "pcol", 0, 0)
    sibling = lax.ppermute(final[:, :64], "prow", SWAP)
    return call(
        finish,
        (shape((2, 4, 64, 256), bf16), shape((2, 256, 256), f32)),
        in_specs=[SMEM, VMEM, VMEM, VMEM],
        out_specs=(VMEM, VMEM),
    )(picks, final, sibling, diag_inverse)


def solution(mesh):
    placed = (P(None, "prow", None, "pcol"), P(None, None, "prow", None), P(), P())
    return jax.shard_map(
        on_device,
        mesh=mesh,
        in_specs=placed,
        out_specs=(P(None, None, ("prow", "pcol"), None), P()),
        check_vma=False,
    )
```

```python
import functools

import jax
import jax.numpy as jnp
from jax import lax
from jax.experimental import pallas as pl
from jax.experimental.pallas import tpu as pltpu
from jax.sharding import PartitionSpec as P

BOTH = ("prow", "pcol")
SMEM = pl.BlockSpec(memory_space=pltpu.SMEM)
VMEM = pl.BlockSpec(memory_space=pltpu.VMEM)
ANY = pl.BlockSpec(memory_space=pl.ANY)
HBM = pl.BlockSpec(memory_space=pltpu.HBM)
VMEM_LIMIT = 48 * 1024 * 1024
SHIFT = (2, 0, 1, 3)


def spread():
    pairs = []
    for row in range(16):
        x, z_hi, core = row // 4, row // 2 % 2, row % 2
        for col in range(8):
            z_lo, y = col // 4, col % 4
            to_x = (x + SHIFT[(y - (z_hi * 2 + core)) % 4]) % 4
            to_z_hi = z_hi if z_lo == x % 2 else 1 - z_hi
            to_row = (to_x * 2 + to_z_hi) * 2 + x // 2
            pairs.append((row * 8 + col, to_row * 8 + row % 8))
    return pairs


SPREAD = spread()
SWAP = [(row, row ^ 1) for row in range(16)]
SAME_CORE = [[row for row in range(16) if row % 2 == core] for core in range(2)]


def pick_blocks(listed, panel, picks, chosen, structure, sems):
    fetch = pltpu.make_async_copy(listed, structure, sems.at[0])
    fetch.start()
    fetch.wait()
    row, col = lax.axis_index("prow"), lax.axis_index("pcol")
    core = row & 1
    wanted = (row, col + 8 * core, col + 8 * (1 - core))
    copies = []
    for s in range(2):
        found = [jnp.int32(0)] * 3
        for k in range(16):
            entry = structure[s, k]
            for i in range(3):
                found[i] += jnp.where((entry & 15) == wanted[i], entry >> 4, 0)
        copies.append(pltpu.make_async_copy(panel.at[s, found[0]], chosen.at[s], sems.at[s]))
        copies[-1].start()
        picks[s, 0] = found[0]
        picks[s, 1] = 2 * found[1] + core
        picks[s, 2] = 2 * found[2] + 1 - core
    for copy in copies:
        copy.wait()


def extract(picks, block, out, wide):
    s = pl.program_id(0)
    rows = block.shape[1]
    for k in range(4):
        lanes = slice(128 * k, 128 * k + 128)
        wide[k] = block[0, :, :, lanes].astype(jnp.float32).reshape(rows * 8, 128)
        for i in range(2):
            column = wide[k, pl.ds(picks[s, 1 + i], rows, stride=8), :]
            out[0, i, :, lanes] = column.astype(jnp.bfloat16)


def multiply(blocks, own, other, out):
    for s in range(2):
        total = None
        for i, factor in enumerate((own, other)):
            term = lax.dot_general(
                factor[s], blocks[s, i], (((0,), (1,)), ((), ())), preferred_element_type=jnp.float32
            )
            total = term if total is None else total + term
        for d in range(8):
            piece = -total[32 * d : 32 * d + 32]
            largest = jnp.max(jnp.max(jnp.abs(piece), axis=0, keepdims=True), axis=1, keepdims=True)
            exponent = jnp.ceil(jnp.log2(jnp.maximum(largest, 2.0**-120)))
            scaled = jnp.clip(piece * jnp.exp2(-exponent) * 32767.0, -32767.0, 32767.0)
            coded = jnp.round(scaled).astype(jnp.int32).astype(jnp.int16)
            for k in range(4):
                row = 64 * k + 32 * s
                out[d, row : row + 32] = coded[:, 128 * k : 128 * k + 128]
            tail = jnp.broadcast_to(exponent, (16, 128)).astype(jnp.int32).astype(jnp.int16)
            out[d, 256 + 16 * s : 272 + 16 * s] = tail


def round_and_project(arrived, chosen, columns, kept, sent):
    core = lax.axis_index("prow") & 1
    for s in range(2):
        total = [jnp.zeros((32, 128), jnp.float32)] * 4
        for i in range(8):
            tail = arrived[i, 256 + 16 * s : 272 + 16 * s].astype(jnp.int32).astype(jnp.float32)
            scale = jnp.exp2(tail[:1]) * (1 / 32767.0)
            for k in range(4):
                row = 64 * k + 32 * s
                coded = arrived[i, row : row + 32].astype(jnp.int32).astype(jnp.float32)
                total[k] += coded * scale
        rounded = jnp.concatenate(total, axis=1).astype(jnp.bfloat16)
        columns[s] = rounded
        term = jnp.dot(rounded, chosen[s], preferred_element_type=jnp.float32)
        first = core == 0
        kept[s] = jnp.where(first, term[:16], term[16:])
        sent[s] = jnp.where(first, term[16:], term[:16])


def pair_sum(kept, arrived, out):
    total = kept[...] + arrived[...]
    for i in range(8):
        out[i] = total


def pack(arrived, columns, out):
    for s in range(2):
        total = arrived[0, s]
        for i in range(1, 8):
            total += arrived[i, s]
        high = total.astype(jnp.bfloat16)
        low = (total - high.astype(jnp.float32)).astype(jnp.bfloat16)
        for i in range(8):
            out[i, 32 * s : 32 * s + 16] = high
            out[i, 32 * s + 16 : 32 * s + 32] = low
            out[i, 64:, 128 * s : 128 * s + 128] = columns[s, :, i // 2 * 128 : i // 2 * 128 + 128]


def finish(picks, own, other, diag_inverse, off_diag, diag_block):
    core = lax.axis_index("prow") & 1
    half = lax.axis_index("pcol") & 1
    off_diag[...] = jnp.zeros_like(off_diag)
    for s in range(2):
        slabs = []
        for i in range(8):
            high, low = (slice(32 * s + 16 * k, 32 * s + 16 * k + 16) for k in range(2))
            mine = own[i, high].astype(jnp.float32) + own[i, low].astype(jnp.float32)
            theirs = other[i, high].astype(jnp.float32) + other[i, low].astype(jnp.float32)
            slabs.append(jnp.where(core == 0, mine, theirs))
            slabs.append(jnp.where(core == 0, theirs, mine))
        diag_block[s] = diag_inverse[s] - jnp.concatenate(slabs, axis=0).T
        part = jnp.concatenate(
            [own[i, 64:, 128 * s : 128 * s + 128].astype(jnp.float32) for i in range(8)], axis=0
        ).T
        rows = jnp.where(half == 0, part[:64], part[64:])
        off_diag[s, picks[s, 0]] = rows.astype(jnp.bfloat16)


def call(body, out_shape, limit=VMEM_LIMIT, **rest):
    return pl.pallas_call(
        body,
        out_shape=out_shape,
        compiler_params=pltpu.CompilerParams(vmem_limit_bytes=limit),
        **rest,
    )


def on_device(inverse, panel, structure, diag_inverse):
    f32, bf16 = jnp.float32, jnp.bfloat16
    shape = jax.ShapeDtypeStruct
    picks, chosen = call(
        pick_blocks,
        (shape((2, 3), jnp.int32), shape((2, 512, 256), bf16)),
        in_specs=[HBM, HBM],
        out_specs=(SMEM, VMEM),
        scratch_shapes=[pltpu.SMEM((2, 16), jnp.int32), pltpu.SemaphoreType.DMA((2,))],
        limit=61 * 1024 * 1024,
    )(structure, panel)
    own = lax.ppermute(chosen, BOTH, SPREAD)
    rows = 128
    blocks = call(
        extract,
        shape((2, 2, 512, 512), bf16),
        grid_spec=pltpu.PrefetchScalarGridSpec(
            num_scalar_prefetch=1,
            grid=(2, 512 // rows),
            in_specs=[pl.BlockSpec((1, rows, 8, 512), lambda s, i, picks: (picks[s, 0], i, 0, 0))],
            out_specs=pl.BlockSpec((1, 2, rows, 512), lambda s, i, picks: (s, 0, i, 0)),
            scratch_shapes=[pltpu.VMEM((4, rows * 8, 128), f32)],
        ),
        cost_estimate=pl.CostEstimate(flops=0, bytes_accessed=10 << 20, transcendentals=0),
    )(picks, inverse)
    own, blocks = lax.optimization_barrier((own, blocks))
    other = lax.ppermute(own, "prow", SWAP)
    partial = call(
        multiply,
        shape((8, 288, 128), jnp.int16),
        in_specs=[VMEM, VMEM, VMEM],
        out_specs=VMEM,
    )(blocks, own, other)
    arrived = lax.all_to_all(partial, "pcol", 0, 0)
    columns, kept, sent = call(
        round_and_project,
        (shape((2, 32, 512), bf16), shape((2, 16, 256), f32), shape((2, 16, 256), f32)),
        in_specs=[VMEM, VMEM],
        out_specs=(VMEM, VMEM, VMEM),
    )(arrived, chosen)
    copies = call(
        pair_sum, shape((8, 2, 16, 256), f32), in_specs=[VMEM, VMEM], out_specs=VMEM
    )(kept, lax.ppermute(sent, "prow", SWAP))
    sums = lax.all_to_all(copies, "prow", 0, 0, axis_index_groups=SAME_CORE)
    packed = call(
        pack, shape((8, 96, 256), bf16), in_specs=[VMEM, VMEM], out_specs=VMEM
    )(sums, columns)
    final = lax.all_to_all(packed, "pcol", 0, 0)
    sibling = lax.ppermute(final[:, :64], "prow", SWAP)
    return call(
        finish,
        (shape((2, 4, 64, 256), bf16), shape((2, 256, 256), f32)),
        in_specs=[SMEM, VMEM, VMEM, VMEM],
        out_specs=(VMEM, VMEM),
    )(picks, final, sibling, diag_inverse)


def solution(mesh):
    placed = (P(None, "prow", None, "pcol"), P(None, None, "prow", None), P(), P())
    return jax.shard_map(
        on_device,
        mesh=mesh,
        in_specs=placed,
        out_specs=(P(None, None, ("prow", "pcol"), None), P()),
        check_vma=False,
    )
```

```python
import functools

import jax
import jax.numpy as jnp
from jax import lax
from jax.experimental import pallas as pl
from jax.experimental.pallas import tpu as pltpu
from jax.sharding import PartitionSpec as P

BOTH = ("prow", "pcol")
SMEM = pl.BlockSpec(memory_space=pltpu.SMEM)
VMEM = pl.BlockSpec(memory_space=pltpu.VMEM)
ANY = pl.BlockSpec(memory_space=pl.ANY)
HBM = pl.BlockSpec(memory_space=pltpu.HBM)
VMEM_LIMIT = 48 * 1024 * 1024
SHIFT = (2, 0, 1, 3)


def spread():
    pairs = []
    for row in range(16):
        x, z_hi, core = row // 4, row // 2 % 2, row % 2
        for col in range(8):
            z_lo, y = col // 4, col % 4
            to_x = (x + SHIFT[(y - (z_hi * 2 + core)) % 4]) % 4
            to_z_hi = z_hi if z_lo == x % 2 else 1 - z_hi
            to_row = (to_x * 2 + to_z_hi) * 2 + x // 2
            pairs.append((row * 8 + col, to_row * 8 + row % 8))
    return pairs


SPREAD = spread()
SWAP = [(row, row ^ 1) for row in range(16)]
SAME_CORE = [[row for row in range(16) if row % 2 == core] for core in range(2)]


def pick_blocks(listed, panel, picks, chosen, structure, sems):
    fetch = pltpu.make_async_copy(listed, structure, sems.at[0])
    fetch.start()
    fetch.wait()
    row, col = lax.axis_index("prow"), lax.axis_index("pcol")
    core = row & 1
    wanted = (row, col + 8 * core, col + 8 * (1 - core))
    lists = [[structure[s, k] for k in range(16)] for s in range(2)]

    def place(s, i):
        return sum(jnp.where((entry & 15) == wanted[i], entry >> 4, 0) for entry in lists[s])

    copies = []
    for s in range(2):
        picks[s, 0] = place(s, 0)
        copies.append(pltpu.make_async_copy(panel.at[s, picks[s, 0]], chosen.at[s], sems.at[s]))
        copies[-1].start()
    for s in range(2):
        picks[s, 1] = 2 * place(s, 1) + core
        picks[s, 2] = 2 * place(s, 2) + 1 - core
    for copy in copies:
        copy.wait()


def extract(picks, block, out, wide):
    s = pl.program_id(0)
    rows = block.shape[1]
    for k in range(4):
        lanes = slice(128 * k, 128 * k + 128)
        wide[k] = block[0, :, :, lanes].astype(jnp.float32).reshape(rows * 8, 128)
        for i in range(2):
            column = wide[k, pl.ds(picks[s, 1 + i], rows, stride=8), :]
            out[0, i, :, lanes] = column.astype(jnp.bfloat16)


def multiply(blocks, own, other, out):
    for s in range(2):
        total = None
        for i, factor in enumerate((own, other)):
            term = lax.dot_general(
                factor[s], blocks[s, i], (((0,), (1,)), ((), ())), preferred_element_type=jnp.float32
            )
            total = term if total is None else total + term
        for d in range(8):
            piece = -total[32 * d : 32 * d + 32]
            largest = jnp.max(jnp.max(jnp.abs(piece), axis=0, keepdims=True), axis=1, keepdims=True)
            exponent = jnp.ceil(jnp.log2(jnp.maximum(largest, 2.0**-120)))
            scaled = jnp.clip(piece * jnp.exp2(-exponent) * 32767.0, -32767.0, 32767.0)
            coded = jnp.round(scaled).astype(jnp.int32).astype(jnp.int16)
            for k in range(4):
                row = 64 * k + 32 * s
                out[d, row : row + 32] = coded[:, 128 * k : 128 * k + 128]
            tail = jnp.broadcast_to(exponent, (16, 128)).astype(jnp.int32).astype(jnp.int16)
            out[d, 256 + 16 * s : 272 + 16 * s] = tail


def round_and_project(arrived, chosen, columns, kept, sent):
    core = lax.axis_index("prow") & 1
    for s in range(2):
        total = [jnp.zeros((32, 128), jnp.float32)] * 4
        for i in range(8):
            tail = arrived[i, 256 + 16 * s : 272 + 16 * s].astype(jnp.int32).astype(jnp.float32)
            scale = jnp.exp2(tail[:1]) * (1 / 32767.0)
            for k in range(4):
                row = 64 * k + 32 * s
                coded = arrived[i, row : row + 32].astype(jnp.int32).astype(jnp.float32)
                total[k] += coded * scale
        rounded = jnp.concatenate(total, axis=1).astype(jnp.bfloat16)
        columns[s] = rounded
        term = jnp.dot(rounded, chosen[s], preferred_element_type=jnp.float32)
        first = core == 0
        kept[s] = jnp.where(first, term[:16], term[16:])
        sent[s] = jnp.where(first, term[16:], term[:16])


def pair_sum(kept, arrived, out):
    total = kept[...] + arrived[...]
    for i in range(8):
        out[i] = total


def pack(arrived, columns, out):
    for s in range(2):
        total = arrived[0, s]
        for i in range(1, 8):
            total += arrived[i, s]
        high = total.astype(jnp.bfloat16)
        low = (total - high.astype(jnp.float32)).astype(jnp.bfloat16)
        for i in range(8):
            out[i, 32 * s : 32 * s + 16] = high
            out[i, 32 * s + 16 : 32 * s + 32] = low
            out[i, 64:, 128 * s : 128 * s + 128] = columns[s, :, i // 2 * 128 : i // 2 * 128 + 128]


def store_rows(picks, final, off_diag):
    half = lax.axis_index("pcol") & 1
    off_diag[...] = jnp.zeros_like(off_diag)
    for s in range(2):
        part = jnp.concatenate(
            [final[i, 64:, 128 * s : 128 * s + 128].astype(jnp.float32) for i in range(8)], axis=0
        ).T
        rows = jnp.where(half == 0, part[:64], part[64:])
        off_diag[s, picks[s, 0]] = rows.astype(jnp.bfloat16)


def store_diag(own, other, diag_inverse, diag_block):
    core = lax.axis_index("prow") & 1
    for s in range(2):
        slabs = []
        for i in range(8):
            high, low = (slice(32 * s + 16 * k, 32 * s + 16 * k + 16) for k in range(2))
            mine = own[i, high].astype(jnp.float32) + own[i, low].astype(jnp.float32)
            theirs = other[i, high].astype(jnp.float32) + other[i, low].astype(jnp.float32)
            slabs.append(jnp.where(core == 0, mine, theirs))
            slabs.append(jnp.where(core == 0, theirs, mine))
        diag_block[s] = diag_inverse[s] - jnp.concatenate(slabs, axis=0).T


def call(body, out_shape, limit=VMEM_LIMIT, **rest):
    return pl.pallas_call(
        body,
        out_shape=out_shape,
        compiler_params=pltpu.CompilerParams(vmem_limit_bytes=limit),
        **rest,
    )


def on_device(inverse, panel, structure, diag_inverse):
    f32, bf16 = jnp.float32, jnp.bfloat16
    shape = jax.ShapeDtypeStruct
    panel = pltpu.with_memory_space_constraint(panel, pltpu.HBM)
    structure = pltpu.with_memory_space_constraint(structure, pltpu.HBM)
    picks, chosen = call(
        pick_blocks,
        (shape((2, 3), jnp.int32), pltpu.VMEM((2, 512, 256), bf16)),
        in_specs=[HBM, HBM],
        out_specs=(SMEM, VMEM),
        scratch_shapes=[pltpu.SMEM((2, 16), jnp.int32), pltpu.SemaphoreType.DMA((2,))],
        limit=32 * 1024 * 1024,
    )(structure, panel)
    own = lax.ppermute(chosen, BOTH, SPREAD)
    rows = 128
    blocks = call(
        extract,
        shape((2, 2, 512, 512), bf16),
        grid_spec=pltpu.PrefetchScalarGridSpec(
            num_scalar_prefetch=1,
            grid=(2, 512 // rows),
            in_specs=[pl.BlockSpec((1, rows, 8, 512), lambda s, i, picks: (picks[s, 0], i, 0, 0))],
            out_specs=pl.BlockSpec((1, 2, rows, 512), lambda s, i, picks: (s, 0, i, 0)),
            scratch_shapes=[pltpu.VMEM((4, rows * 8, 128), f32)],
        ),
        cost_estimate=pl.CostEstimate(flops=0, bytes_accessed=10 << 20, transcendentals=0),
    )(picks, inverse)
    own, blocks = lax.optimization_barrier((own, blocks))
    other = lax.ppermute(own, "prow", SWAP)
    partial = call(
        multiply,
        shape((8, 288, 128), jnp.int16),
        in_specs=[VMEM, VMEM, VMEM],
        out_specs=VMEM,
    )(blocks, own, other)
    arrived = lax.all_to_all(partial, "pcol", 0, 0)
    columns, kept, sent = call(
        round_and_project,
        (shape((2, 32, 512), bf16), shape((2, 16, 256), f32), shape((2, 16, 256), f32)),
        in_specs=[VMEM, VMEM],
        out_specs=(VMEM, VMEM, VMEM),
    )(arrived, chosen)
    copies = call(
        pair_sum, shape((8, 2, 16, 256), f32), in_specs=[VMEM, VMEM], out_specs=VMEM
    )(kept, lax.ppermute(sent, "prow", SWAP))
    sums = lax.all_to_all(copies, "prow", 0, 0, axis_index_groups=SAME_CORE)
    packed = call(
        pack, shape((8, 96, 256), bf16), in_specs=[VMEM, VMEM], out_specs=VMEM
    )(sums, columns)
    final = lax.all_to_all(packed, "pcol", 0, 0)
    sibling = lax.ppermute(final[:, :64], "prow", SWAP)
    off_diag = call(
        store_rows, shape((2, 4, 64, 256), bf16), in_specs=[SMEM, VMEM], out_specs=VMEM
    )(picks, final)
    diag_block = call(
        store_diag, shape((2, 256, 256), f32), in_specs=[VMEM, VMEM, VMEM], out_specs=VMEM
    )(final, sibling, diag_inverse)
    return off_diag, diag_block


def solution(mesh):
    placed = (P(None, "prow", None, "pcol"), P(None, None, "prow", None), P(), P())
    return jax.shard_map(
        on_device,
        mesh=mesh,
        in_specs=placed,
        out_specs=(P(None, None, ("prow", "pcol"), None), P()),
        check_vma=False,
    )
```

```python
import functools

import jax
import jax.numpy as jnp
from jax import lax
from jax.experimental import pallas as pl
from jax.experimental.pallas import tpu as pltpu
from jax.sharding import PartitionSpec as P

BOTH = ("prow", "pcol")
SMEM = pl.BlockSpec(memory_space=pltpu.SMEM)
VMEM = pl.BlockSpec(memory_space=pltpu.VMEM)
ANY = pl.BlockSpec(memory_space=pl.ANY)
HBM = pl.BlockSpec(memory_space=pltpu.HBM)
VMEM_LIMIT = 48 * 1024 * 1024
SHIFT = (2, 0, 1, 3)


def spread():
    pairs = []
    for row in range(16):
        x, z_hi, core = row // 4, row // 2 % 2, row % 2
        for col in range(8):
            z_lo, y = col // 4, col % 4
            to_x = (x + SHIFT[(y - (z_hi * 2 + core)) % 4]) % 4
            to_z_hi = z_hi if z_lo == x % 2 else 1 - z_hi
            to_row = (to_x * 2 + to_z_hi) * 2 + x // 2
            pairs.append((row * 8 + col, to_row * 8 + row % 8))
    return pairs


SPREAD = spread()
SWAP = [(row, row ^ 1) for row in range(16)]
SAME_CORE = [[row for row in range(16) if row % 2 == core] for core in range(2)]


def pick_blocks(listed, panel, picks, chosen, structure, table, candidates, sems):
    fetch = pltpu.make_async_copy(listed, structure, sems.at[2])
    fetch.start()
    copies = [pltpu.make_async_copy(panel.at[s], candidates.at[s], sems.at[s]) for s in range(2)]
    for copy in copies:
        copy.start()
    fetch.wait()
    row, col = lax.axis_index("prow"), lax.axis_index("pcol")
    core = row & 1
    wanted = (row, col + 8 * core, col + 8 * (1 - core))
    for s in range(2):
        for k in range(16):
            entry = structure[s, k]
            table[s, entry & 15] = entry >> 4
    for s in range(2):
        picks[s, 0] = table[s, row]
        picks[s, 1] = 2 * table[s, wanted[1]] + core
        picks[s, 2] = 2 * table[s, wanted[2]] + 1 - core
    for s in range(2):
        copies[s].wait()
        chosen[s] = candidates[s, table[s, row]]


def extract(picks, block, out, wide):
    s = pl.program_id(0)
    rows = block.shape[1]
    for k in range(4):
        lanes = slice(128 * k, 128 * k + 128)
        wide[k] = block[0, :, :, lanes].astype(jnp.float32).reshape(rows * 8, 128)
        for i in range(2):
            column = wide[k, pl.ds(picks[s, 1 + i], rows, stride=8), :]
            out[0, i, :, lanes] = column.astype(jnp.bfloat16)


def to_code(piece):
    largest = jnp.max(jnp.max(jnp.abs(piece), axis=0, keepdims=True), axis=1, keepdims=True)
    exponent = jnp.ceil(jnp.log2(jnp.maximum(largest, 2.0**-120)))
    scaled = jnp.clip(piece * jnp.exp2(-exponent) * 32767.0, -32767.0, 32767.0)
    return jnp.round(scaled).astype(jnp.int32).astype(jnp.int16), exponent


def from_code(coded, tail):
    scale = jnp.exp2(tail.astype(jnp.int32).astype(jnp.float32)) * (1 / 32767.0)
    return coded.astype(jnp.int32).astype(jnp.float32) * scale


def tail_of(exponents, lanes):
    lane = lax.broadcasted_iota(jnp.int32, (8, lanes), 1) // (lanes // len(exponents))
    tail = jnp.zeros((8, lanes), jnp.float32)
    for i, exponent in enumerate(exponents):
        tail = jnp.where(lane == i, exponent, tail)
    return tail.astype(jnp.int32).astype(jnp.int16)


def multiply(blocks, own, other, out):
    exponents = [[] for _ in range(8)]
    for s in range(2):
        total = None
        for i, factor in enumerate((own, other)):
            term = lax.dot_general(
                factor[s], blocks[s, i], (((0,), (1,)), ((), ())), preferred_element_type=jnp.float32
            )
            total = term if total is None else total + term
        for d in range(8):
            coded, exponent = to_code(-total[32 * d : 32 * d + 32])
            exponents[d].append(exponent)
            for k in range(4):
                row = 64 * k + 32 * s
                out[d, row : row + 32] = coded[:, 128 * k : 128 * k + 128]
    for d in range(8):
        out[d, 256:] = tail_of(exponents[d], 128)


def round_and_project(arrived, chosen, columns, kept, sent):
    first = (lax.axis_index("prow") & 1) == 0
    for s in range(2):
        parts = []
        for k in range(4):
            row = 64 * k + 32 * s
            total = jnp.zeros((32, 128), jnp.float32)
            for i in range(8):
                total += from_code(arrived[i, row : row + 32], arrived[i, 256:257, 64 * s : 64 * s + 1])
            parts.append(total)
        total = jnp.concatenate(parts, axis=1)
        columns[s] = total
        term = jnp.dot(total.astype(jnp.bfloat16), chosen[s], preferred_element_type=jnp.float32)
        kept[s] = jnp.where(first, term[:16], term[16:])
        sent[s] = jnp.where(first, term[16:], term[:16])


def pair_sum(kept, arrived, out):
    coded, exponents = zip(*[to_code(kept[s] + arrived[s]) for s in range(2)])
    tail = tail_of(exponents, 128)
    for i in range(8):
        for s in range(2):
            out[i, 32 * s : 32 * s + 16] = coded[s][:, :128]
            out[i, 32 * s + 16 : 32 * s + 32] = coded[s][:, 128:]
        out[i, 64:] = tail


def pack(arrived, columns, out):
    exponents, whole = [], []
    for s in range(2):
        parts = []
        for k in range(2):
            row = 32 * s + 16 * k
            total = jnp.zeros((16, 128), jnp.float32)
            for i in range(8):
                total += from_code(arrived[i, row : row + 16], arrived[i, 64:65, 64 * s : 64 * s + 1])
            parts.append(total)
        coded, exponent = to_code(jnp.concatenate(parts, axis=1))
        exponents.append(exponent)
        for i in range(8):
            out[i, 16 * s : 16 * s + 16] = coded
    for s in range(2):
        coded, exponent = to_code(columns[s])
        exponents.append(exponent)
        whole.append(coded.astype(jnp.int32).astype(jnp.float32))
    tail = tail_of(exponents, 256)
    for i in range(8):
        piece = jnp.concatenate([part[:, 64 * i : 64 * i + 64] for part in whole], axis=1)
        piece = jnp.concatenate([piece[:16], piece[16:]], axis=1)
        out[i, 32:40] = tail
        out[i, 40:] = piece.astype(jnp.int32).astype(jnp.int16)


def store_rows(picks, final, off_diag):
    left = lax.broadcasted_iota(jnp.int32, (1, 128), 1) < 64
    slabs = []
    for i in range(8):
        tail = jnp.where(left, final[i, 32:33, 128:129].astype(jnp.int32), final[i, 32:33, 192:193].astype(jnp.int32))
        scale = jnp.exp2(tail.astype(jnp.float32)) * (1 / 32767.0)
        coded = final[i, 40:].astype(jnp.int32).astype(jnp.float32)
        slabs += [coded[:, :128] * scale, coded[:, 128:] * scale]
    rows = jnp.concatenate(slabs, axis=0).T
    for s in range(2):
        for r in range(4):
            off_diag[s, r] = jnp.where(picks[s : s + 1, :1] == r, rows[64 * s : 64 * s + 64], 0.0).astype(jnp.bfloat16)


def store_diag(own, other, diag_inverse, diag_block):
    first = (lax.axis_index("prow") & 1) == 0
    for s in range(2):
        rows, lane = slice(16 * s, 16 * s + 16), slice(64 * s, 64 * s + 1)
        slabs = []
        for i in range(8):
            mine = from_code(own[i, rows], own[i, 32:33, lane])
            theirs = from_code(other[i, rows], other[i, 32:33, lane])
            slabs += [jnp.where(first, mine, theirs), jnp.where(first, theirs, mine)]
        diag_block[s] = diag_inverse[s] - jnp.concatenate(slabs, axis=0).T


def call(body, out_shape, limit=VMEM_LIMIT, **rest):
    return pl.pallas_call(
        body,
        out_shape=out_shape,
        compiler_params=pltpu.CompilerParams(vmem_limit_bytes=limit),
        **rest,
    )


def on_device(inverse, panel, structure, diag_inverse):
    f32, bf16, i16 = jnp.float32, jnp.bfloat16, jnp.int16
    shape = jax.ShapeDtypeStruct
    panel = pltpu.with_memory_space_constraint(panel, pltpu.HBM)
    structure = pltpu.with_memory_space_constraint(structure, pltpu.HBM)
    picks, chosen = call(
        pick_blocks,
        (shape((2, 3), jnp.int32), pltpu.VMEM((2, 512, 256), bf16)),
        in_specs=[HBM, HBM],
        out_specs=(SMEM, VMEM),
        scratch_shapes=[
            pltpu.SMEM((2, 16), jnp.int32),
            pltpu.SMEM((2, 16), jnp.int32),
            pltpu.VMEM((2, 4, 512, 256), bf16),
            pltpu.SemaphoreType.DMA((3,)),
        ],
        limit=32 * 1024 * 1024,
    )(structure, panel)
    own = lax.ppermute(chosen, BOTH, SPREAD)
    rows = 128
    blocks = call(
        extract,
        shape((2, 2, 512, 512), bf16),
        grid_spec=pltpu.PrefetchScalarGridSpec(
            num_scalar_prefetch=1,
            grid=(2, 512 // rows),
            in_specs=[pl.BlockSpec((1, rows, 8, 512), lambda s, i, picks: (picks[s, 0], i, 0, 0))],
            out_specs=pl.BlockSpec((1, 2, rows, 512), lambda s, i, picks: (s, 0, i, 0)),
            scratch_shapes=[pltpu.VMEM((4, rows * 8, 128), f32)],
        ),
        cost_estimate=pl.CostEstimate(flops=0, bytes_accessed=10 << 20, transcendentals=0),
    )(picks, inverse)
    own, blocks = lax.optimization_barrier((own, blocks))
    other = lax.ppermute(own, "prow", SWAP)
    partial = call(
        multiply,
        shape((8, 264, 128), i16),
        in_specs=[VMEM, VMEM, VMEM],
        out_specs=VMEM,
    )(blocks, own, other)
    arrived = lax.all_to_all(partial, "pcol", 0, 0)
    columns, kept, sent = call(
        round_and_project,
        (shape((2, 32, 512), f32), shape((2, 16, 256), f32), shape((2, 16, 256), f32)),
        in_specs=[VMEM, VMEM],
        out_specs=(VMEM, VMEM, VMEM),
    )(arrived, chosen)
    copies = call(pair_sum, shape((8, 72, 128), i16), in_specs=[VMEM, VMEM], out_specs=VMEM)(
        kept, lax.ppermute(sent, "prow", SWAP)
    )
    sums = lax.all_to_all(copies, "prow", 0, 0, axis_index_groups=SAME_CORE)
    packed = call(pack, shape((8, 56, 256), i16), in_specs=[VMEM, VMEM], out_specs=VMEM)(sums, columns)
    final = lax.all_to_all(packed, "pcol", 0, 0)
    sibling = lax.ppermute(final[:, :40], "prow", SWAP)
    off_diag = call(
        store_rows, shape((2, 4, 64, 256), bf16), in_specs=[VMEM, VMEM], out_specs=VMEM
    )(picks, final)
    diag_block = call(
        store_diag, shape((2, 256, 256), f32), in_specs=[VMEM, VMEM, VMEM], out_specs=VMEM
    )(final, sibling, diag_inverse)
    return off_diag, diag_block


def solution(mesh):
    placed = (P(None, "prow", None, "pcol"), P(None, None, "prow", None), P(), P())
    return jax.shard_map(
        on_device,
        mesh=mesh,
        in_specs=placed,
        out_specs=(P(None, None, ("prow", "pcol"), None), P()),
        check_vma=False,
    )
```

```python
import functools

import jax
import jax.numpy as jnp
from jax import lax
from jax.experimental import pallas as pl
from jax.experimental.pallas import tpu as pltpu
from jax.sharding import PartitionSpec as P

BOTH = ("prow", "pcol")
SMEM = pl.BlockSpec(memory_space=pltpu.SMEM)
VMEM = pl.BlockSpec(memory_space=pltpu.VMEM)
ANY = pl.BlockSpec(memory_space=pl.ANY)
HBM = pl.BlockSpec(memory_space=pltpu.HBM)
VMEM_LIMIT = 48 * 1024 * 1024
SHIFT = (2, 0, 1, 3)


def spread():
    pairs = []
    for row in range(16):
        x, z_hi, core = row // 4, row // 2 % 2, row % 2
        for col in range(8):
            z_lo, y = col // 4, col % 4
            to_x = (x + SHIFT[(y - (z_hi * 2 + core)) % 4]) % 4
            to_z_hi = z_hi if z_lo == x % 2 else 1 - z_hi
            to_row = (to_x * 2 + to_z_hi) * 2 + x // 2
            pairs.append((row * 8 + col, to_row * 8 + row % 8))
    return pairs


SPREAD = spread()
SWAP = [(row, row ^ 1) for row in range(16)]
SAME_CORE = [[row for row in range(16) if row % 2 == core] for core in range(2)]


def pick_blocks(listed, panel, picks, chosen, structure, table, candidates, sems):
    fetch = pltpu.make_async_copy(listed, structure, sems.at[2])
    fetch.start()
    copies = [pltpu.make_async_copy(panel.at[s], candidates.at[s], sems.at[s]) for s in range(2)]
    for copy in copies:
        copy.start()
    fetch.wait()
    row, col = lax.axis_index("prow"), lax.axis_index("pcol")
    core = row & 1
    wanted = (row, col + 8 * core, col + 8 * (1 - core))
    for s in range(2):
        for k in range(16):
            entry = structure[s, k]
            table[s, entry & 15] = entry >> 4
    for s in range(2):
        picks[s, 0] = table[s, row]
        picks[s, 1] = 2 * table[s, wanted[1]] + core
        picks[s, 2] = 2 * table[s, wanted[2]] + 1 - core
    for s in range(2):
        copies[s].wait()
        chosen[s] = candidates[s, table[s, row]]


def extract(picks, block, out, wide):
    s = pl.program_id(0)
    rows = block.shape[1]
    for k in range(4):
        lanes = slice(128 * k, 128 * k + 128)
        wide[k] = block[0, :, :, lanes].astype(jnp.float32).reshape(rows * 8, 128)
        for i in range(2):
            column = wide[k, pl.ds(picks[s, 1 + i], rows, stride=8), :]
            out[0, i, :, lanes] = column.astype(jnp.bfloat16)


def to_code(piece):
    largest = jnp.max(jnp.max(jnp.abs(piece), axis=0, keepdims=True), axis=1, keepdims=True)
    exponent = jnp.ceil(jnp.log2(jnp.maximum(largest, 2.0**-120)))
    scaled = jnp.clip(piece * jnp.exp2(-exponent) * 32767.0, -32767.0, 32767.0)
    return jnp.round(scaled).astype(jnp.int32).astype(jnp.int16), exponent


def from_code(coded, tail):
    scale = jnp.exp2(tail.astype(jnp.int32).astype(jnp.float32)) * (1 / 32767.0)
    return coded.astype(jnp.int32).astype(jnp.float32) * scale


def tail_of(exponents, lanes):
    lane = lax.broadcasted_iota(jnp.int32, (8, lanes), 1) // (lanes // len(exponents))
    tail = jnp.zeros((8, lanes), jnp.float32)
    for i, exponent in enumerate(exponents):
        tail = jnp.where(lane == i, exponent, tail)
    return tail.astype(jnp.int32).astype(jnp.int16)


def multiply(blocks, own, other, out):
    exponents = [[] for _ in range(8)]
    for s in range(2):
        total = None
        for i, factor in enumerate((own, other)):
            term = lax.dot_general(
                factor[s], blocks[s, i], (((0,), (1,)), ((), ())), preferred_element_type=jnp.float32
            )
            total = term if total is None else total + term
        for d in range(8):
            coded, exponent = to_code(-total[32 * d : 32 * d + 32])
            exponents[d].append(exponent)
            for k in range(4):
                row = 64 * k + 32 * s
                out[d, row : row + 32] = coded[:, 128 * k : 128 * k + 128]
    for d in range(8):
        out[d, 256:] = tail_of(exponents[d], 128)


def round_and_project(arrived, chosen, columns, kept, sent):
    first = (lax.axis_index("prow") & 1) == 0
    for s in range(2):
        parts = []
        for k in range(4):
            row = 64 * k + 32 * s
            total = jnp.zeros((32, 128), jnp.float32)
            for i in range(8):
                total += from_code(arrived[i, row : row + 32], arrived[i, 256:257, 64 * s : 64 * s + 1])
            parts.append(total)
        total = jnp.concatenate(parts, axis=1)
        columns[s] = total
        term = jnp.dot(total.astype(jnp.bfloat16), chosen[s], preferred_element_type=jnp.float32)
        kept[s] = jnp.where(first, term[:16], term[16:])
        sent[s] = jnp.where(first, term[16:], term[:16])


def pair_sum(kept, arrived, out):
    coded, exponents = zip(*[to_code(kept[s] + arrived[s]) for s in range(2)])
    tail = tail_of(exponents, 128)
    for i in range(8):
        for s in range(2):
            out[i, 32 * s : 32 * s + 16] = coded[s][:, :128]
            out[i, 32 * s + 16 : 32 * s + 32] = coded[s][:, 128:]
        out[i, 64:] = tail


def pack(arrived, columns, out):
    exponents, whole = [], []
    for s in range(2):
        parts = []
        for k in range(2):
            row = 32 * s + 16 * k
            total = jnp.zeros((16, 128), jnp.float32)
            for i in range(8):
                total += from_code(arrived[i, row : row + 16], arrived[i, 64:65, 64 * s : 64 * s + 1])
            parts.append(total)
        coded, exponent = to_code(jnp.concatenate(parts, axis=1))
        exponents.append(exponent)
        for i in range(8):
            out[i, 16 * s : 16 * s + 16] = coded
    for s in range(2):
        coded, exponent = to_code(columns[s])
        exponents.append(exponent)
        whole.append(coded.astype(jnp.int32).astype(jnp.float32))
    tail = tail_of(exponents, 256)
    for i in range(8):
        piece = jnp.concatenate([part[:, 64 * i : 64 * i + 64] for part in whole], axis=1)
        piece = jnp.concatenate([piece[:16], piece[16:]], axis=1)
        out[i, 32:40] = tail
        out[i, 40:] = piece.astype(jnp.int32).astype(jnp.int16)


def store_rows(picks, final, off_diag):
    left = lax.broadcasted_iota(jnp.int32, (1, 128), 1) < 64
    slabs = []
    for i in range(8):
        tail = jnp.where(left, final[i, 32:33, 128:129].astype(jnp.int32), final[i, 32:33, 192:193].astype(jnp.int32))
        scale = jnp.exp2(tail.astype(jnp.float32)) * (1 / 32767.0)
        coded = final[i, 40:].astype(jnp.int32).astype(jnp.float32)
        slabs += [coded[:, :128] * scale, coded[:, 128:] * scale]
    rows = jnp.concatenate(slabs, axis=0).T
    for s in range(2):
        for r in range(4):
            off_diag[s, r] = jnp.where(picks[s : s + 1, :1] == r, rows[64 * s : 64 * s + 64], 0.0).astype(jnp.bfloat16)


def store_diag(own, other, diag_inverse, diag_block, result, sems):
    first = (lax.axis_index("prow") & 1) == 0
    copies = []
    for s in range(2):
        rows, lane = slice(16 * s, 16 * s + 16), slice(64 * s, 64 * s + 1)
        slabs = []
        for i in range(8):
            mine = from_code(own[i, rows], own[i, 32:33, lane])
            theirs = from_code(other[i, rows], other[i, 32:33, lane])
            slabs += [jnp.where(first, mine, theirs), jnp.where(first, theirs, mine)]
        result[s] = diag_inverse[s] - jnp.concatenate(slabs, axis=0).T
        copies.append(pltpu.make_async_copy(result.at[s], diag_block.at[s], sems.at[s]))
        copies[-1].start()
    for copy in copies:
        copy.wait()


def call(body, out_shape, limit=VMEM_LIMIT, **rest):
    return pl.pallas_call(
        body,
        out_shape=out_shape,
        compiler_params=pltpu.CompilerParams(vmem_limit_bytes=limit),
        **rest,
    )


def on_device(inverse, panel, structure, diag_inverse):
    f32, bf16, i16 = jnp.float32, jnp.bfloat16, jnp.int16
    shape = jax.ShapeDtypeStruct
    panel = pltpu.with_memory_space_constraint(panel, pltpu.HBM)
    structure = pltpu.with_memory_space_constraint(structure, pltpu.HBM)
    picks, chosen = call(
        pick_blocks,
        (shape((2, 3), jnp.int32), pltpu.VMEM((2, 512, 256), bf16)),
        in_specs=[HBM, HBM],
        out_specs=(SMEM, VMEM),
        scratch_shapes=[
            pltpu.SMEM((2, 16), jnp.int32),
            pltpu.SMEM((2, 16), jnp.int32),
            pltpu.VMEM((2, 4, 512, 256), bf16),
            pltpu.SemaphoreType.DMA((3,)),
        ],
        limit=32 * 1024 * 1024,
    )(structure, panel)
    own = lax.ppermute(chosen, BOTH, SPREAD)
    rows = 128
    blocks = call(
        extract,
        shape((2, 2, 512, 512), bf16),
        grid_spec=pltpu.PrefetchScalarGridSpec(
            num_scalar_prefetch=1,
            grid=(2, 512 // rows),
            in_specs=[pl.BlockSpec((1, rows, 8, 512), lambda s, i, picks: (picks[s, 0], i, 0, 0))],
            out_specs=pl.BlockSpec((1, 2, rows, 512), lambda s, i, picks: (s, 0, i, 0)),
            scratch_shapes=[pltpu.VMEM((4, rows * 8, 128), f32)],
        ),
        cost_estimate=pl.CostEstimate(flops=0, bytes_accessed=10 << 20, transcendentals=0),
    )(picks, inverse)
    own, blocks = lax.optimization_barrier((own, blocks))
    other = lax.ppermute(own, "prow", SWAP)
    partial = call(
        multiply,
        shape((8, 264, 128), i16),
        in_specs=[VMEM, VMEM, VMEM],
        out_specs=VMEM,
    )(blocks, own, other)
    arrived = lax.all_to_all(partial, "pcol", 0, 0)
    columns, kept, sent = call(
        round_and_project,
        (shape((2, 32, 512), f32), shape((2, 16, 256), f32), shape((2, 16, 256), f32)),
        in_specs=[VMEM, VMEM],
        out_specs=(VMEM, VMEM, VMEM),
    )(arrived, chosen)
    copies = call(pair_sum, shape((8, 72, 128), i16), in_specs=[VMEM, VMEM], out_specs=VMEM)(
        kept, lax.ppermute(sent, "prow", SWAP)
    )
    sums = lax.all_to_all(copies, "prow", 0, 0, axis_index_groups=SAME_CORE)
    packed = call(pack, shape((8, 56, 256), i16), in_specs=[VMEM, VMEM], out_specs=VMEM)(sums, columns)
    final = lax.all_to_all(packed, "pcol", 0, 0)
    sibling = lax.ppermute(final[:, :40], "prow", SWAP)
    off_diag = call(
        store_rows, shape((2, 4, 64, 256), bf16), in_specs=[VMEM, VMEM], out_specs=VMEM
    )(picks, final)
    diag_block = call(
        store_diag,
        shape((2, 256, 256), f32),
        in_specs=[VMEM, VMEM, VMEM],
        out_specs=HBM,
        scratch_shapes=[pltpu.VMEM((2, 256, 256), f32), pltpu.SemaphoreType.DMA((2,))],
    )(final, sibling, diag_inverse)
    return off_diag, diag_block


def solution(mesh):
    placed = (P(None, "prow", None, "pcol"), P(None, None, "prow", None), P(), P())
    return jax.shard_map(
        on_device,
        mesh=mesh,
        in_specs=placed,
        out_specs=(P(None, None, ("prow", "pcol"), None), P()),
        check_vma=False,
    )
```
